32 devices in a mesh: seq: 4 (over y, x), head: 4 (over z), rep: 2 (over core).
Axes of the slice: x: 2, y: 2, z: 4, core: 2. Of those that a mesh axis runs over, the one named last changes fastest.
Arguments:
- query_heads: bfloat16 [2, 8192, 4096], P('rep', 'seq', 'head'), may hold values from -0.59765625 to 0.59765625
- key_heads: bfloat16 [2, 8192, 4096], P('rep', 'seq', 'head'), may hold values from -0.59765625 to 0.59765625
- value_heads: bfloat16 [2, 8192, 4096], P('rep', 'seq', 'head'), may hold values from -6 to 6
- out_cotangent: bfloat16 [2, 8192, 4096], P('rep', 'seq', 'head'), may hold values from -0.19921875 to 0.19921875
- out_weight: bfloat16 [4096, 4096], P('head'), may hold values from -0.09375 to 0.09375
- doc_ends: int32 [2, 7], P('rep'), may hold values from 1 to 8192, as said below
Outputs:
- grad_query: bfloat16 [2, 8192, 4096], P('rep', 'seq', 'head')
- grad_key: bfloat16 [2, 8192, 4096], P('rep', 'seq', 'head')
- grad_value: bfloat16 [2, 8192, 4096], P('rep', 'seq', 'head')
- grad_weight: float32 [4096, 4096], P('head', ('seq', 'rep'))
The draws below stay inside these ranges and needn't reach their ends.
Inputs may be any that keep to these rules, and one draw needn't show every extreme that they name: `doc_ends`: each row holds 7 strictly increasing document end offsets; its last entry is 8192.
All inputs are finite; a program needn't handle non-finite values.
Results may differ from the reference program's by a relative error of at most 0.0052.
Values may be sent and summed in bfloat16 or wider, within the bound.
No kernel may reach another device: no remote copies, remote signals or barrier semaphores. Data moves between devices by JAX's collectives and lax.ppermute only.
A program may use at most 320 MiB of HBM per device.

```python
import jax
import jax.numpy as jnp
from jax import lax

D = 4096
HD = 128
H = 32
BLOCK = 512
SEQ = 8192
BATCH = 2
DOCS = 7


def draw_doc_ends(key, part):
    row_keys = jax.random.split(jax.random.fold_in(key, 11), BATCH)

    def one_row(row_key):
        order = jax.random.permutation(row_key, SEQ - 1).astype(jnp.int32) + 1
        cuts = jnp.sort(order[:DOCS - 1])
        return jnp.concatenate([cuts, jnp.full((1,), SEQ, jnp.int32)]).astype(jnp.int32)
    return jax.vmap(one_row)(row_keys)


def strengthened(result, key, source, target, parts, factor):
    owner, partner = [(jnp.arange(result.shape[axis_at]) // (result.shape[axis_at] // parts)).reshape([-1 if axis == axis_at else 1 for axis in range(result.ndim)]) for axis_at in (source, target)]
    chosen = jax.random.permutation(key, parts)[partner]
    strong = (owner == chosen) | (owner == (partner + parts // 2) % parts)
    return jnp.where(strong, factor * result, result)


def steps_of(stream_key, dims, cuts, smallest, high):
    def one(dim, shards_of):
        draws = jax.random.uniform(jax.random.fold_in(jax.random.fold_in(stream_key, 6), dim), (shards_of,), jnp.float32, smallest / len(cuts), high / len(cuts))
        return jnp.repeat(jnp.exp(draws), dims[dim] // shards_of).reshape((-1,) + (1,) * (len(dims) - dim - 1))

    gain = one(*cuts[0])
    for cut in cuts[1:]:
        gain = gain * one(*cut)
    return gain


def noise(rng, extent, deviation, bound, shards=(), held_as=jnp.bfloat16):
    drawn = deviation * jax.random.normal(rng, extent, jnp.float32)
    if shards:
        drawn = drawn * steps_of(rng, extent, shards, -0.22, 0.18)
    return jnp.clip(drawn, -bound, bound).astype(held_as)


def gaussian_with(rng, dims, scale, reach, cuts, heavy, kind=jnp.bfloat16):
    entries = scale * jax.random.normal(rng, dims, jnp.float32)
    if cuts:
        entries = entries * steps_of(rng, dims, cuts, -0.22, 0.18)
    return jnp.clip(strengthened(entries, jax.random.fold_in(rng, 3), *heavy), -reach, reach).astype(kind)


def setup_inputs(seed: int = 0) -> dict:
    splits = jax.random.split(jax.random.key(seed), 7)
    return {
        "query_heads": noise(splits[0], (BATCH, SEQ, H * HD), 0.1, 0.59765625, ((0, 2), (1, 4), (2, 4))),
        "key_heads": noise(splits[1], (BATCH, SEQ, H * HD), 0.1, 0.59765625, ((0, 2), (1, 4), (2, 4))),
        "value_heads": noise(splits[2], (BATCH, SEQ, H * HD), 1.0, 6.0, ((0, 2), (1, 4), (2, 4))),
        "out_cotangent": gaussian_with(splits[3], (BATCH, SEQ, D), 0.03125, 0.19921875, ((0, 2), (1, 4), (2, 4)), (1, 2, 4, 2.0)),
        "out_weight": noise(splits[4], (H * HD, D), (H * HD) ** -0.5, 0.09375, ((0, 4),)),
        "doc_ends": draw_doc_ends(jax.random.fold_in(splits[6], 71), 0),
    }


highest = lax.Precision.HIGHEST


def doc_counts(positions, ends_row):
    return jnp.sum((ends_row[None, :] <= positions[:, None]).astype(jnp.int32), axis=1)


def multiply(form, left, right):
    return jnp.einsum(form, left.astype(jnp.float32), right.astype(jnp.float32))


def local_pass(queries, keys, values, grads, counts, count_before):
    length, heads, width = queries.shape
    blocks = length // BLOCK
    query_blocks = queries.reshape(blocks, BLOCK, heads, width)
    key_blocks = keys.reshape(blocks, BLOCK, heads, width)
    value_blocks = values.reshape(blocks, BLOCK, heads, width)
    grad_blocks = grads.reshape(blocks, BLOCK, heads, width)
    count_blocks = counts.reshape(blocks, BLOCK)
    before_each = jnp.concatenate([jnp.reshape(count_before, (1,)).astype(jnp.int32), count_blocks[:-1, -1]])
    last_each = count_blocks[:, -1]
    rows = lax.broadcasted_iota(jnp.int32, (BLOCK, BLOCK), 0)
    cols = lax.broadcasted_iota(jnp.int32, (BLOCK, BLOCK), 1)
    allowed = ((count_blocks[:, :, None] == count_blocks[:, None, :]) & (rows >= cols)[None]).astype(jnp.float32)
    scores = multiply("nthe,nshe->nhts", query_blocks, key_blocks)
    attn = lax.optimization_barrier((scores * allowed[:, None]).astype(jnp.bfloat16))
    back = multiply("nthe,nshe->nhts", grad_blocks, value_blocks)
    pgrad = lax.optimization_barrier((back * allowed[:, None]).astype(jnp.bfloat16))
    out_intra = multiply("nhts,nshe->nthe", attn, value_blocks)
    dq_intra = multiply("nhts,nshe->nthe", pgrad, key_blocks)
    dk_intra = multiply("nhts,nthe->nshe", pgrad, query_blocks)
    dv_intra = multiply("nhts,nthe->nshe", attn, grad_blocks)
    first_match = (count_blocks == before_each[:, None]).astype(jnp.float32)[:, :, None, None]
    last_match = (count_blocks == last_each[:, None]).astype(jnp.float32)[:, :, None, None]
    keep = (last_each == before_each).astype(jnp.float32)
    tails = multiply("nshe,nshf->nhef", key_blocks.astype(jnp.float32) * last_match, value_blocks)
    head_sums = multiply("nthe,nthf->nhef", query_blocks.astype(jnp.float32) * first_match, grad_blocks)

    def link_step(state, item):
        return item[0] + item[1] * state, state

    empty = jnp.zeros((heads, width, width), jnp.float32)
    final_tail, states_before = lax.scan(link_step, empty, (tails, keep))
    final_head, states_after = lax.scan(link_step, empty, (head_sums, keep), reverse=True)
    outputs = out_intra + first_match * jnp.einsum("nthe,nhef->nthf", query_blocks.astype(jnp.float32), states_before, precision=highest)
    dq = dq_intra + first_match * jnp.einsum("nthf,nhef->nthe", grad_blocks.astype(jnp.float32), states_before, precision=highest)
    dk = dk_intra + last_match * jnp.einsum("nshf,nhef->nshe", value_blocks.astype(jnp.float32), states_after, precision=highest)
    dv = dv_intra + last_match * jnp.einsum("nshe,nhef->nshf", key_blocks.astype(jnp.float32), states_after, precision=highest)
    shape = (length, heads, width)
    return outputs.reshape(shape), dq.reshape(shape), dk.reshape(shape), dv.reshape(shape), final_tail, final_head


def reference(query_heads, key_heads, value_heads, out_cotangent, out_weight, doc_ends):
    batch, length, flat = query_heads.shape
    heads = flat // HD
    total = jnp.zeros((flat, out_cotangent.shape[2]), jnp.float32)
    grad_q, grad_k, grad_v = [], [], []
    for row in range(batch):
        grads = jnp.dot(out_cotangent[row], out_weight.T, preferred_element_type=jnp.float32).astype(jnp.bfloat16)
        grads = lax.optimization_barrier(grads)
        counts = doc_counts(jnp.arange(length, dtype=jnp.int32), doc_ends[row])

        def split(array):
            return array.reshape(length, heads, HD).transpose(1, 0, 2)[:, :, None, :]

        def per_head(items):
            return local_pass(items[0], items[1], items[2], items[3], counts, jnp.zeros((), jnp.int32))

        outputs, dq, dk, dv, tails, head_sums = lax.map(per_head, (split(query_heads[row]), split(key_heads[row]), split(value_heads[row]), split(grads)))

        def join(array):
            return array[:, :, 0, :].transpose(1, 0, 2).reshape(length, flat).astype(jnp.bfloat16)

        attn_out = join(outputs)
        total = total + jnp.dot(attn_out.T, out_cotangent[row], preferred_element_type=jnp.float32)
        grad_q.append(join(dq))
        grad_k.append(join(dk))
        grad_v.append(join(dv))
    return jnp.stack(grad_q), jnp.stack(grad_k), jnp.stack(grad_v), total
```

```python
import functools

import jax
import jax.numpy as jnp
from jax import lax
from jax.experimental import pallas as pl
from jax.experimental.pallas import tpu as pltpu
from jax.sharding import PartitionSpec as P


HD = 128
TB = 256
bf16 = jnp.bfloat16
f32 = jnp.float32


def nn(a, b):
    return lax.dot_general(a, b, (((1,), (0,)), ((), ())), preferred_element_type=f32)


def nt(a, b):
    return lax.dot_general(a, b, (((1,), (1,)), ((), ())), preferred_element_type=f32)


def tn(a, b):
    return lax.dot_general(a, b, (((0,), (0,)), ((), ())), preferred_element_type=f32)


def doc_start(info, docs, at):
    start = jnp.zeros_like(at)
    for i in range(docs):
        end = info[i]
        start = jnp.where(end <= at, end, start)
    return start


def col_iota(first):
    return first + lax.broadcasted_iota(jnp.int32, (TB, HD), 0)


def tail_kernel(info, a_ref, b_ref, out_ref, *, docs, heads, of_last):
    step = pl.program_id(0)

    @pl.when(step == 0)
    def _():
        out_ref[...] = jnp.zeros_like(out_ref)

    base = info[docs]
    first = base + step * TB
    at = col_iota(first)
    if of_last:
        match = at >= doc_start(info, docs, base + info[docs + 1] - 1)
    else:
        match = doc_start(info, docs, at) < base
    weight = match.astype(bf16)
    for h in range(heads):
        cols = slice(h * HD, (h + 1) * HD)
        out_ref[h] += tn(a_ref[:, cols] * weight, b_ref[:, cols])


def block_terms(info, docs, first):
    at = col_iota(first)
    start = doc_start(info, docs, at)
    last_start = doc_start(info, docs, first + TB - 1)
    first_match = start < first
    last_match = at >= last_start
    keep = jnp.where(last_start < first, 1.0, 0.0).astype(f32)
    return start, first_match, last_match, keep


def lower_mask(start, first):
    rows = lax.broadcasted_iota(jnp.int32, (TB, TB), 0)
    cols = lax.broadcasted_iota(jnp.int32, (TB, TB), 1)
    from_ = jnp.concatenate([start - first] * (TB // HD), axis=1)
    return (cols <= rows) & (cols >= from_)


def upper_mask(info, docs, first):
    rows = lax.broadcasted_iota(jnp.int32, (TB, TB), 0)
    cols = lax.broadcasted_iota(jnp.int32, (TB, TB), 1)
    start = doc_start(info, docs, first + lax.broadcasted_iota(jnp.int32, (1, TB), 1)) - first
    return (rows <= cols) & (rows >= start)


def forward_kernel(info, x_ref, k_ref, v_ref, carry_ref, *refs, docs, heads, flip, steps):
    outs, state = refs[:-1], refs[-1]
    step = pl.program_id(0)

    @pl.when(step == 0)
    def _():
        state[...] = carry_ref[...]

    first = info[docs] + step * TB
    start, first_match, last_match, keep = block_terms(info, docs, first)
    mask = lower_mask(start, first)
    first_weight = first_match.astype(bf16)
    last_weight = last_match.astype(bf16)
    for h in range(heads):
        cols = slice(h * HD, (h + 1) * HD)
        x, k, v = x_ref[:, cols], k_ref[:, cols], v_ref[:, cols]
        now = state[h]
        if flip:
            inner = jnp.where(mask, nt(x, v), 0.0).astype(bf16)
            out = nn(inner, k) + nt(x * first_weight, now.astype(bf16))
        else:
            inner = jnp.where(mask, nt(x, k), 0.0).astype(bf16)
            out = nn(inner, v) + nn(x * first_weight, now.astype(bf16))
        state[h] = keep * now + tn(k * last_weight, v)
        if flip:
            outs[0][:, cols] = out.astype(bf16)
            continue
        turned = out.T.astype(bf16)
        each = steps // len(outs)
        for i, out_ref in enumerate(outs):
            @pl.when(step // each == i)
            def _():
                out_ref[cols, :] = turned


def backward_kernel(info, q_ref, k_ref, v_ref, g_ref, carry_ref, dk_ref, dv_ref, state, *, docs, heads, steps):
    step = pl.program_id(0)

    @pl.when(step == 0)
    def _():
        state[...] = carry_ref[...]

    first = info[docs] + (steps - 1 - step) * TB
    _, first_match, last_match, keep = block_terms(info, docs, first)
    mask = upper_mask(info, docs, first)
    first_weight = first_match.astype(bf16)
    last_weight = last_match.astype(bf16)
    for h in range(heads):
        cols = slice(h * HD, (h + 1) * HD)
        q, k, v, g = q_ref[:, cols], k_ref[:, cols], v_ref[:, cols], g_ref[:, cols]
        now = state[h]
        low = now.astype(bf16)
        attn = jnp.where(mask, nt(k, q), 0.0).astype(bf16)
        pgrad = jnp.where(mask, nt(v, g), 0.0).astype(bf16)
        dk_ref[:, cols] = (nn(pgrad, q) + nt(v * last_weight, low)).astype(bf16)
        dv_ref[:, cols] = (nn(attn, g) + nn(k * last_weight, low)).astype(bf16)
        state[h] = keep * now + tn(q * first_weight, g)


def params():
    return pltpu.CompilerParams(dimension_semantics=("arbitrary",))


def cost(length, heads, matmuls, states, arrays):
    flops = length * heads * 2 * HD * (matmuls * TB + states * HD)
    return pl.CostEstimate(flops=flops, bytes_accessed=arrays * length * heads * HD * 2, transcendentals=0)


def device_state(info, a, b, docs, of_last):
    length, width = a.shape
    heads = width // HD
    spec = pl.BlockSpec((TB, width), lambda i, info: (i, 0))
    whole = pl.BlockSpec((heads, HD, HD), lambda i, info: (0, 0, 0))
    return pl.pallas_call(
        functools.partial(tail_kernel, docs=docs, heads=heads, of_last=of_last),
        out_shape=jax.ShapeDtypeStruct((heads, HD, HD), f32),
        grid_spec=pltpu.PrefetchScalarGridSpec(
            num_scalar_prefetch=1, grid=(length // TB,), in_specs=[spec, spec], out_specs=whole),
        compiler_params=params(), cost_estimate=cost(length, heads, 0, 1, 2),
    )(info, a, b)


def forward(info, x, k, v, carry, docs, flip, parts=1):
    length, width = x.shape
    heads = width // HD
    steps = length // TB
    each = steps // parts
    spec = pl.BlockSpec((TB, width), lambda i, info: (i, 0))
    whole = pl.BlockSpec((heads, HD, HD), lambda i, info: (0, 0, 0))
    if flip:
        out_shape, out_specs = (jax.ShapeDtypeStruct((length, width), bf16),), [spec]
    else:
        out_shape = (jax.ShapeDtypeStruct((width, length // parts), bf16),) * parts
        out_specs = [
            pl.BlockSpec((width, TB), lambda i, info, j=j: (0, jnp.clip(i - j * each, 0, each - 1)))
            for j in range(parts)]
    return pl.pallas_call(
        functools.partial(forward_kernel, docs=docs, heads=heads, flip=flip, steps=steps),
        out_shape=out_shape,
        grid_spec=pltpu.PrefetchScalarGridSpec(
            num_scalar_prefetch=1, grid=(steps,), in_specs=[spec, spec, spec, whole], out_specs=out_specs,
            scratch_shapes=[pltpu.VMEM((heads, HD, HD), f32)]),
        compiler_params=params(), cost_estimate=cost(length, heads, 2, 2, 4),
    )(info, x, k, v, carry)


def backward(info, q, k, v, g, carry, docs):
    length, width = q.shape
    heads = width // HD
    steps = length // TB
    spec = pl.BlockSpec((TB, width), lambda i, info: (steps - 1 - i, 0))
    whole = pl.BlockSpec((heads, HD, HD), lambda i, info: (0, 0, 0))
    return pl.pallas_call(
        functools.partial(backward_kernel, docs=docs, heads=heads, steps=steps),
        out_shape=(jax.ShapeDtypeStruct((length, width), bf16),) * 2,
        grid_spec=pltpu.PrefetchScalarGridSpec(
            num_scalar_prefetch=1, grid=(steps,), in_specs=[spec] * 4 + [whole], out_specs=[spec, spec],
            scratch_shapes=[pltpu.VMEM((heads, HD, HD), f32)]),
        compiler_params=params(), cost_estimate=cost(length, heads, 4, 3, 6), name="grad_kv",
    )(info, q, k, v, g, carry)


def carried(state, weights, before):
    count = lax.axis_size("seq")
    low = state.astype(bf16)
    total = jnp.zeros_like(state)
    for gap in range(1, count):
        if before:
            pairs = [(j, j + gap) for j in range(count - gap)]
        else:
            pairs = [(j + gap, j) for j in range(count - gap)]
        moved = lax.ppermute(low, "seq", pairs)
        total = total + weights[gap - 1] * moved.astype(f32)
    return total


def spread_kernel(at, *refs, terms, sums, outs):
    xs, ws = refs[:terms[0]], refs[terms[0]:terms[0] + terms[1]]
    bases = refs[terms[0] + terms[1]:-len(outs)]
    out_refs = refs[-len(outs):]
    for out_ref, products, base in zip(out_refs, outs, sums):
        total = None
        for i, j in products:
            term = nt(xs[i][...], ws[j][...])
            total = term if total is None else total + term
        for b in base:
            total = total + bases[b][...].astype(f32)
        out_ref[...] = total.astype(out_ref.dtype)


def spread(xs, ws, bases, outs, dtype, into=None, offset=0, size=None, block=512):
    depth = xs[0][0].shape[1]
    width = ws[0][0].shape[0]
    size = size or xs[0][0].shape[0]
    block = min(block, size)
    steps = size // block
    cols = jnp.stack([jnp.asarray(d, jnp.int32) for _, d in ws])
    x_specs = [pl.BlockSpec((block, depth), lambda i, at, f=f: (i + f, 0)) for _, f in xs]
    w_specs = [pl.BlockSpec((width, depth), lambda i, at, j=j: (0, at[j])) for j in range(len(ws))]
    b_specs = [pl.BlockSpec((block, width), lambda i, at, f=f: (i + f, 0)) for _, f in bases]
    length = size if into is None else into[0]
    out_spec = pl.BlockSpec((block, width), lambda i, at: (i + offset, 0))
    operands = [x for x, _ in xs] + [w for w, _ in ws] + [b for b, _ in bases]
    in_specs = x_specs + w_specs + b_specs
    alias = {}
    body = functools.partial(
        spread_kernel, terms=(len(xs), len(ws)), sums=[o[1] for o in outs], outs=[o[0] for o in outs])
    kernel = body
    if into is not None and into[1] is not None:
        alias = {1 + len(operands): 0}
        operands.append(into[1])
        in_specs = in_specs + [pl.BlockSpec(memory_space=pl.ANY)]
        extra = len(operands)

        def kernel(at, *refs):
            return body(at, *(refs[:extra - 1] + refs[extra:]))

    flops = sum(len(o[0]) for o in outs) * 2 * size * depth * width
    moved = 2 * (len(xs) * size * depth + len(ws) * width * depth) + 4 * (len(outs) + len(bases)) * size * width
    return pl.pallas_call(
        kernel,
        out_shape=tuple(jax.ShapeDtypeStruct((length, width), dtype) for _ in outs),
        grid_spec=pltpu.PrefetchScalarGridSpec(
            num_scalar_prefetch=1, grid=(steps,), in_specs=in_specs, out_specs=[out_spec] * len(outs)),
        compiler_params=params(), input_output_aliases=alias,
        cost_estimate=pl.CostEstimate(flops=flops, bytes_accessed=moved, transcendentals=0),
    )(cols, *operands)


def gather_kernel(*refs, lefts, parts):
    left, right, out_ref = refs[:lefts], refs[lefts:-1], refs[-1]
    total = None
    for i in range(parts):
        a, b = left[i * lefts // parts], right[i * len(right) // parts]
        ka, kb = a.shape[1] * lefts // parts, b.shape[0] * len(right) // parts
        ia, ib = i % (parts // lefts), i % (parts // len(right))
        term = nn(a[:, ia * ka:(ia + 1) * ka], b[ib * kb:(ib + 1) * kb, :])
        total = term if total is None else total + term
    out_ref[...] = total.astype(out_ref.dtype)


def weight_term(lefts, rights, block=256):
    width = lefts[0].shape[0]
    depth = rights[0].shape[1]
    block = min(block, depth)
    length = sum(x.shape[1] for x in lefts)
    return pl.pallas_call(
        functools.partial(gather_kernel, lefts=len(lefts), parts=max(len(lefts), len(rights))),
        out_shape=jax.ShapeDtypeStruct((width, depth), bf16),
        grid=(depth // block,),
        in_specs=[pl.BlockSpec(x.shape, lambda i: (0, 0)) for x in lefts]
        + [pl.BlockSpec((x.shape[0], block), lambda i: (0, i)) for x in rights],
        out_specs=pl.BlockSpec((width, block), lambda i: (0, i)),
        compiler_params=params(),
        cost_estimate=pl.CostEstimate(
            flops=2 * length * width * depth, bytes_accessed=2 * length * (width + depth), transcendentals=0),
    )(*lefts, *rights)


def row_start(ends, at):
    return jnp.max(jnp.where(ends <= at, ends, 0))


def gather_plan(c, w, values_of, rest_of):
    full = lax.all_gather(c, "head", axis=1, tiled=True)
    (attn_out,) = values_of(1)
    grads = nt(full, w).astype(bf16)
    outs = rest_of(grads)
    partial = nn(attn_out, full).astype(bf16)
    grad_w = lax.psum_scatter(partial, ("seq", "rep"), scatter_dimension=1, tiled=True)
    return outs, grad_w.astype(f32)


SWAP = [(0, 1), (1, 0), (2, 3), (3, 2)]
MIDDLE = [(1, 2), (2, 1)]
OUTWARD = [(1, 0), (2, 3)]
INWARD = [(0, 1), (3, 2)]


def line_plan(c, w, values_of, rest_of, pieces=4):
    me = lax.axis_index("head")
    length, depth = c.shape
    rows = w.shape[0]
    group = ("seq", "rep")
    count = lax.axis_size(group)
    part = rows // count

    def send(x, pairs):
        return lax.ppermute(x, "head", pairs)

    def scatter(x):
        return lax.psum_scatter(x, group, scatter_dimension=0, tiled=True)

    def columns(x, d):
        return lax.dynamic_slice_in_dim(x, d * depth, depth, 1)

    d_own, d_one, d_two, d_three = me, me ^ 1, 3 - me, (3 - me) ^ 1
    mine = lax.dynamic_slice_in_dim(w, lax.axis_index(group) * part, part, 0)
    far_w = jnp.concatenate([columns(mine, d_three), columns(mine, d_two)], axis=1)
    far_w = send(far_w, INWARD)
    far_w = lax.all_gather(far_w, group, axis=0, tiled=True)

    one = send(c, SWAP)
    two = send(c, MIDDLE)
    step = length // pieces
    three = [send(one[i * step:(i + 1) * step], MIDDLE) for i in range(pieces)]

    (own_sum,) = spread([(c, 0)], [(w, d_own)], [], [([(0, 0)], [])], f32)
    attn_out = values_of(2)
    far_out = [send(x, INWARD) for x in attn_out]
    terms = [weight_term(attn_out, [c])]
    near_sum, far_sum = spread(
        [(one, 0), (two, 0)], [(w, d_one), (w, d_two), (far_w, 0)], [(own_sum, 0)],
        [([(0, 0), (1, 1)], [0]), ([(1, 2)], [])], f32)
    terms += [weight_term(attn_out, [one]), weight_term(attn_out, [two])]
    far_grads = []
    for i in range(pieces):
        (x,) = spread([(three[i], 0)], [(far_w, 1)], [(far_sum, i)], [([(0, 0)], [0])], bf16)
        far_grads.append(send(x, OUTWARD))
    terms += [
        weight_term(attn_out, three),
        weight_term(far_out, [two]), weight_term(far_out, three)]
    grads = None
    for i in range(pieces):
        (grads,) = spread(
            [(three[i], 0)], [(w, d_three)], [(near_sum, i), (far_grads[i], 0)],
            [([(0, 0)], [0, 1])], bf16, into=(length, grads), offset=i)
    outs = rest_of(grads)

    terms = [scatter(x) for x in terms]
    sent = [send(x, OUTWARD) for x in terms[4:]]
    total = jnp.zeros((part, 4 * depth), bf16)
    for d, term in ((d_own, terms[0]), (d_one, terms[1]), (d_two, terms[2] + sent[1]), (d_three, terms[3] + sent[0])):
        total = lax.dynamic_update_slice_in_dim(total, term, d * depth, 1)
    grad_w = lax.all_to_all(total, group, split_axis=1, concat_axis=0, tiled=True)
    return outs, grad_w.astype(f32)


def on_device(query_heads, key_heads, value_heads, out_cotangent, out_weight, doc_ends):
    q, k, v, c = query_heads[0], key_heads[0], value_heads[0], out_cotangent[0]
    length = q.shape[0]
    ends = doc_ends[0].astype(jnp.int32)
    docs = ends.shape[0]
    here, count = lax.axis_index("seq"), lax.axis_size("seq")
    first = here * length
    last = first + length - 1
    info = jnp.concatenate([ends, jnp.stack([first, jnp.full_like(first, length)])]).astype(jnp.int32)

    before_start = row_start(ends, first - 1)
    before = [(before_start <= last - gap * length).astype(f32) for gap in range(1, count)]
    after = [(row_start(ends, first + gap * length - 1) <= last).astype(f32) for gap in range(1, count)]

    held = []

    def values_of(parts):
        tail = device_state(info, k, v, docs, True)
        held.append(carried(tail, before, True))
        return forward(info, q, k, v, held[0], docs, False, parts)

    def rest_of(grads):
        head = device_state(info, q, grads, docs, False)
        carry = carried(head, after, False)
        (dq,) = forward(info, grads, k, v, held[0], docs, True)
        dk, dv = backward(info, q, k, v, grads, carry, docs)
        return dq[None], dk[None], dv[None]

    plan = line_plan if lax.axis_size("head") == 4 else gather_plan
    outs, grad_w = plan(c, out_weight, values_of, rest_of)
    return outs + (grad_w,)


def solution(mesh):
    in_specs = (
        P("rep", "seq", "head"),
        P("rep", "seq", "head"),
        P("rep", "seq", "head"),
        P("rep", "seq", "head"),
        P("head", None),
        P("rep", None),
    )
    out_specs = (
        P("rep", "seq", "head"),
        P("rep", "seq", "head"),
        P("rep", "seq", "head"),
        P("head", ("seq", "rep")),
    )

    return jax.shard_map(on_device, mesh=mesh, in_specs=in_specs, out_specs=out_specs, check_vma=False)
```
